32 devices in a mesh: groups: 2 (over y), seq: 16 (over z, x, core).
Axes of the slice: x: 2, y: 2, z: 4, core: 2. Of those that a mesh axis runs over, the one named last changes fastest.
Arguments:
- queries: bfloat16 [4096, 24, 128], P(('groups', 'seq')), parts along dimension 0, may hold values from -72 to 72
- key_heads: bfloat16 [4096, 4, 128], P(('groups', 'seq')), parts along dimension 0, may hold values from -4 to 4
- value_heads: bfloat16 [4096, 4, 128], P(('groups', 'seq')), parts along dimension 0, may hold values from -6 to 6
- grad_out: bfloat16 [4096, 24, 128], P(('groups', 'seq')), parts along dimension 0, may hold values from -6 to 6
- offsets: int32 [2], replicated, may hold values from 1 to 8, as said below
- random_masks: int32 [1], replicated, may hold values from 1 to 15
- global_blocks: int32 [1], replicated, may hold values from 0 to 15
Outputs:
- attended: bfloat16 [4096, 24, 128], P(('groups', 'seq')), parts along dimension 0
- grad_queries: bfloat16 [4096, 24, 128], P(('groups', 'seq')), parts along dimension 0
- grad_keys: bfloat16 [4096, 4, 128], P(('groups', 'seq')), parts along dimension 0
- grad_values: bfloat16 [4096, 4, 128], P(('groups', 'seq')), parts along dimension 0
The draws below stay inside these ranges and needn't reach their ends.
There are 2 independent parts, one for each index of `groups`. The reference program is written for one: setup_inputs(seed, part) draws one part's arguments, and reference() takes and returns one part's arrays. A program takes and returns all parts, laid end to end along the dimension named above; an argument that names none is the same for every part. Nothing has to cross between parts.
Inputs may be any that keep to these rules, and one draw needn't show every extreme that they name: `offsets`: distinct powers of two; one of them is 8.
All inputs are finite; a program needn't handle non-finite values.
Results may differ from the reference program's by a relative error of at most 0.012.
Values may be sent and summed in bfloat16 or wider, within the bound.
No kernel may reach another device: no remote copies, remote signals or barrier semaphores. Data moves between devices by JAX's collectives and lax.ppermute only.
A program may use at most 64 MiB of HBM per device.

```python
import jax
import jax.numpy as jnp
from jax import lax

HEADS = 24
KVH = 4
HD = 128
BLK = 128
LEVELS = 2
RAND = 1
GLOB = 1
NBLK = 16
TOKENS = 2048
GROUPED = 6


def shared_keys(key):
    base = jnp.clip(jax.random.normal(jax.random.fold_in(key, 11), (NBLK, BLK, KVH, HD), jnp.float32), -4.0, 4.0)
    return base


def draw_key_heads(key, part):
    return shared_keys(key).reshape(TOKENS, KVH, HD).astype(jnp.bfloat16)


def draw_queries(key, part):
    noise = jnp.clip(jax.random.normal(jax.random.fold_in(key, 23), (NBLK, BLK, HEADS, HD), jnp.float32), -4.0, 4.0)
    return noise.reshape(TOKENS, HEADS, HD).astype(jnp.bfloat16)


def draw_offsets(key, part):
    width_bits = NBLK.bit_length() - 1
    lower = jax.random.permutation(jax.random.fold_in(key, 31), width_bits - 1)[:LEVELS - 1].astype(jnp.int32)
    chosen = jnp.concatenate([lower, jnp.full((1,), width_bits - 1, jnp.int32)])
    chosen = jax.random.permutation(jax.random.fold_in(key, 37), chosen).astype(jnp.int32)
    return jnp.left_shift(jnp.ones((LEVELS,), jnp.int32), chosen)


def shard_levels(own_key, shape, pieces, smallest, high):
    loudness, own = 1.0, jax.random.fold_in(own_key, 6)
    for dim, blocks in pieces:
        heights = jnp.exp(jax.random.uniform(jax.random.fold_in(own, dim), (blocks,), jnp.float32, smallest / len(pieces), high / len(pieces)))
        loudness = loudness * jnp.repeat(heights, shape[dim] // blocks).reshape([-1 if axis == dim else 1 for axis in range(len(shape))])
    return loudness


def centred(stream_key, dims, deviation, most, shards=(), held_as=jnp.bfloat16):
    values = deviation * jax.random.normal(stream_key, dims, jnp.float32)
    if shards:
        values = values * shard_levels(stream_key, dims, shards, -0.22, 0.18)
    return jnp.clip(values, -most, most).astype(held_as)


def setup_inputs(seed: int = 0, part: int = 0) -> dict:
    seeds = jax.random.split(jax.random.key(seed), 8)
    own_keys = jax.random.split(jax.random.fold_in(seeds[7], part), 8)
    return {
        "queries": draw_queries(jax.random.fold_in(jax.random.fold_in(seeds[7], part), 71), part),
        "key_heads": draw_key_heads(jax.random.fold_in(jax.random.fold_in(seeds[7], part), 71), part),
        "value_heads": centred(own_keys[2], (TOKENS, KVH, HD), 1.0, 6.0, ((0, 16),)),
        "grad_out": centred(own_keys[3], (TOKENS, HEADS, HD), 1.0, 6.0, ((0, 16),)),
        "offsets": draw_offsets(jax.random.fold_in(seeds[7], 71), part),
        "random_masks": jax.random.randint(seeds[5], (RAND,), 1, NBLK).astype(jnp.int32),
        "global_blocks": jax.random.randint(seeds[6], (GLOB,), 0, NBLK).astype(jnp.int32),
    }


def forward_head(query_part, key_part, value_part):
    scale = query_part.shape[-1] ** -0.5
    scores = jnp.einsum('qpd,kd->pqk', query_part.astype(jnp.float32), key_part.astype(jnp.float32)) * scale
    top_score = jnp.max(scores, axis=-1, keepdims=True)
    log_total = top_score[..., 0] + jnp.log(jnp.sum(jnp.exp(scores - top_score), axis=-1))
    probs = jnp.exp(scores - log_total[..., None]).astype(jnp.bfloat16)
    output_part = jnp.einsum('pqk,kd->qpd', probs.astype(jnp.float32), value_part.astype(jnp.float32))
    return output_part.astype(jnp.bfloat16), log_total


def backward_head(query_part, key_part, value_part, grad_part, output_part, log_total):
    scale = query_part.shape[-1] ** -0.5
    scores = jnp.einsum('qpd,kd->pqk', query_part.astype(jnp.float32), key_part.astype(jnp.float32)) * scale
    weights = jnp.exp(scores - log_total[..., None])
    probs = weights.astype(jnp.bfloat16)
    deltas = jnp.sum(grad_part.astype(jnp.float32) * output_part.astype(jnp.float32), axis=-1).T
    value_terms = jnp.einsum('pqk,qpd->kd', probs.astype(jnp.float32), grad_part.astype(jnp.float32))
    grad_probs = jnp.einsum('qpd,kd->pqk', grad_part.astype(jnp.float32), value_part.astype(jnp.float32))
    grad_scores = (weights * (grad_probs - deltas[..., None])).astype(jnp.bfloat16)
    grad_query = jnp.einsum('pqk,kd->qpd', grad_scores.astype(jnp.float32), key_part.astype(jnp.float32)) * scale
    key_terms = jnp.einsum('pqk,qpd->kd', grad_scores.astype(jnp.float32), query_part.astype(jnp.float32)) * scale
    return grad_query.astype(jnp.bfloat16), key_terms, value_terms


def reference(queries, key_heads, value_heads, grad_out, offsets, random_masks, global_blocks):
    query_blocks = queries.reshape(NBLK, BLK, KVH, GROUPED, HD)
    grad_blocks = grad_out.reshape(NBLK, BLK, KVH, GROUPED, HD)
    key_blocks = key_heads.reshape(NBLK, BLK, KVH, HD)
    value_blocks = value_heads.reshape(NBLK, BLK, KVH, HD)
    listed = 1 + LEVELS + RAND + GLOB

    def visit(totals, block):
        block = block.astype(jnp.int32)
        chosen = jnp.concatenate([block[None], jnp.bitwise_xor(block, offsets), jnp.bitwise_xor(block, random_masks), global_blocks]).astype(jnp.int32)
        keys_all = key_blocks[chosen].reshape(listed * BLK, KVH, HD).transpose(1, 0, 2)
        values_all = value_blocks[chosen].reshape(listed * BLK, KVH, HD).transpose(1, 0, 2)
        query_part = query_blocks[block].transpose(1, 0, 2, 3)
        grad_part = grad_blocks[block].transpose(1, 0, 2, 3)
        output_part, log_total = jax.vmap(forward_head)(query_part, keys_all, values_all)
        grad_query, key_terms, value_terms = jax.vmap(backward_head)(query_part, keys_all, values_all, grad_part, output_part, log_total)
        terms = jnp.stack([key_terms, value_terms]).reshape(2, KVH, listed, BLK, HD).transpose(2, 0, 3, 1, 4)
        totals = totals.at[chosen].add(terms)
        return totals, (output_part.transpose(1, 0, 2, 3), grad_query.transpose(1, 0, 2, 3))

    start = jnp.zeros((NBLK, 2, BLK, KVH, HD), jnp.float32)
    totals, (outputs, grads) = lax.scan(visit, start, jnp.arange(NBLK, dtype=jnp.int32))
    attended = outputs.reshape(TOKENS, HEADS, HD)
    grad_queries = grads.reshape(TOKENS, HEADS, HD)
    grad_keys = totals[:, 0].reshape(TOKENS, KVH, HD).astype(jnp.bfloat16)
    grad_values = totals[:, 1].reshape(TOKENS, KVH, HD).astype(jnp.bfloat16)
    return (attended, grad_queries, grad_keys, grad_values)
```

```python
import functools

import jax
import jax.numpy as jnp
from jax import lax
from jax.experimental import pallas as pl
from jax.experimental.pallas import tpu as pltpu
from jax.sharding import PartitionSpec as P

DIGIT = 4


def exchange(x, mask):
    size = lax.axis_size("seq")
    return lax.ppermute(x, "seq", [(i, i ^ mask) for i in range(size)])


def route(x, mask):
    bits = lax.axis_size("seq").bit_length() - 1
    for low in range(0, bits, DIGIT):
        width = min(DIGIT, bits - low)
        digit = jnp.bitwise_and(jnp.right_shift(mask, low), (1 << width) - 1)
        moves = [lambda t: t] + [
            lambda t, m=value << low: exchange(t, m) for value in range(1, 1 << width)
        ]
        x = lax.switch(digit, moves, x)
    return x


def bit_of(x, bit):
    return jnp.bitwise_and(jnp.right_shift(x, bit), 1)


def higher_bits():
    bits = lax.axis_size("seq").bit_length() - 1
    return list(range(bits - 1, 0, -1))


def fetch_global(own, source):
    me = lax.axis_index("seq")
    even = bit_of(me, 0) == 0
    kept = jnp.where(even, own[0], own[1])
    given = jnp.where(even, own[1], own[0])
    half = jnp.where(bit_of(me, 0) == bit_of(source, 0), kept, exchange(given, 1))
    for bit in higher_bits():
        other = exchange(half, 1 << bit)
        half = jnp.where(bit_of(me, bit) == bit_of(source, bit), half, other)
    other = exchange(half, 1)
    return jnp.stack([jnp.where(even, half, other), jnp.where(even, other, half)])


def reduce_global(terms, target):
    me = lax.axis_index("seq")
    even = bit_of(me, 0) == 0
    kept = jnp.where(even, terms[0], terms[1])
    given = jnp.where(even, terms[1], terms[0])
    half = kept + exchange(given.astype(jnp.bfloat16), 1).astype(jnp.float32)
    for bit in higher_bits():
        other = exchange(half.astype(jnp.bfloat16), 1 << bit).astype(jnp.float32)
        half = half + jnp.where(bit_of(me, bit) == bit_of(target, bit), other, 0.0)
    other = exchange(half.astype(jnp.bfloat16), 1).astype(jnp.float32)
    total = jnp.stack([jnp.where(even, half, other), jnp.where(even, other, half)])
    return jnp.where(me == target, total, 0.0)


def attention_kernel(
    near_count, which_ref, q_ref, g_ref, own_ref, far_ref, rand_ref, glob_ref, *rest
):
    near_refs = rest[:near_count]
    out_ref, dq_ref, own_t, far_t, near_t, rand_t, glob_t = rest[near_count:]
    group, rows, width = q_ref.shape
    scale = width**-0.5
    which = which_ref[0]

    def listed(side):
        near = near_refs[0][side, 0]
        for bit in range(1, near_count):
            near = jnp.where(which == bit, near_refs[bit][side, 0], near)
        return jnp.concatenate(
            [own_ref[side, 0], far_ref[side, 0], near, rand_ref[side, 0], glob_ref[side, 0]]
        )

    keys, values = listed(0), listed(1)
    q = q_ref[...].reshape(group * rows, width)
    g = g_ref[...].reshape(group * rows, width)
    contract_last = (((1,), (1,)), ((), ()))
    contract_first = (((0,), (0,)), ((), ()))
    scores = (
        lax.dot_general(keys, q, contract_last, preferred_element_type=jnp.float32) * scale
    )
    top = jnp.max(scores, axis=0, keepdims=True)
    weights = jnp.exp(scores - top)
    weights = weights * (1.0 / jnp.sum(weights, axis=0, keepdims=True))
    probs = weights.astype(jnp.bfloat16)
    out_t = lax.dot_general(values, probs, contract_first, preferred_element_type=jnp.float32)
    out = out_t.T.astype(jnp.bfloat16)
    out_ref[...] = out.reshape(group, rows, width)
    deltas = jnp.sum(
        g.T.astype(jnp.float32) * out_t.astype(jnp.bfloat16).astype(jnp.float32),
        axis=0,
        keepdims=True,
    )
    grad_probs = lax.dot_general(values, g, contract_last, preferred_element_type=jnp.float32)
    grad_scores = (weights * (grad_probs - deltas)).astype(jnp.bfloat16)
    dq_t = lax.dot_general(keys, grad_scores, contract_first, preferred_element_type=jnp.float32)
    dq_ref[...] = (dq_t * scale).T.astype(jnp.bfloat16).reshape(group, rows, width)
    key_terms = jnp.dot(grad_scores, q, preferred_element_type=jnp.float32) * scale
    value_terms = jnp.dot(probs, g, preferred_element_type=jnp.float32)
    for place, ref in enumerate((own_t, far_t, near_t, rand_t, glob_t)):
        part = slice(place * rows, (place + 1) * rows)
        ref[0, 0] = key_terms[part].astype(ref.dtype)
        ref[1, 0] = value_terms[part].astype(ref.dtype)


def attention(which, q, g, own, far, rand, glob, near):
    heads, rows, width = q.shape
    kv_count = own.shape[1]
    group = heads // kv_count
    by_query = pl.BlockSpec((group, rows, width), lambda h, *_: (h, 0, 0))
    by_key = pl.BlockSpec((2, 1, rows, width), lambda h, *_: (0, h, 0, 0))
    queries = jax.ShapeDtypeStruct(q.shape, q.dtype)
    exact = jax.ShapeDtypeStruct(own.shape, jnp.float32)
    sent = jax.ShapeDtypeStruct(own.shape, jnp.bfloat16)
    flops = 12 * heads * rows * 5 * rows * width
    return pl.pallas_call(
        functools.partial(attention_kernel, len(near)),
        grid_spec=pltpu.PrefetchScalarGridSpec(
            num_scalar_prefetch=1,
            grid=(kv_count,),
            in_specs=[by_query] * 2 + [by_key] * (4 + len(near)),
            out_specs=[by_query] * 2 + [by_key] * 5,
        ),
        out_shape=[queries, queries, exact, sent, sent, sent, exact],
        cost_estimate=pl.CostEstimate(
            flops=flops, bytes_accessed=8 * q.size, transcendentals=5 * rows * rows * heads
        ),
        name="attention",
    )(which, q, g, own, far, rand, glob, *near)


def local(queries, key_heads, value_heads, grad_out, offsets, random_masks, global_blocks):
    size = lax.axis_size("seq")
    me = lax.axis_index("seq")
    half = size // 2
    near_bits = size.bit_length() - 2
    other = jnp.where(offsets[0] == half, offsets[1], offsets[0])
    which = sum((other >= (2 << bit)).astype(jnp.int32) for bit in range(near_bits))
    mask, source = random_masks[0], global_blocks[0]

    own = jnp.stack([key_heads, value_heads]).transpose(0, 2, 1, 3)
    far = exchange(own, half)
    near = [exchange(own, 1 << bit) for bit in range(near_bits)]
    glob = fetch_global(own, source)
    rand = route(own, mask)
    q = queries.transpose(1, 0, 2)
    g = grad_out.transpose(1, 0, 2)
    out, dq, own_t, far_t, near_t, rand_t, glob_t = attention(
        which[None], q, g, own, far, rand, glob, near
    )
    rand_in = route(rand_t, mask)
    far_in = exchange(far_t, half)
    near_in = [exchange(near_t, 1 << bit) for bit in range(near_bits)]
    picked = near_in[0]
    for bit in range(1, near_bits):
        picked = jnp.where(which == bit, near_in[bit], picked)
    totals = own_t + reduce_global(glob_t, source)
    for part in (far_in, picked, rand_in):
        totals = totals + part.astype(jnp.float32)
    grads = totals.astype(jnp.bfloat16).transpose(0, 2, 1, 3)
    return (out.transpose(1, 0, 2), dq.transpose(1, 0, 2), grads[0], grads[1])


def solution(mesh):
    split = P(("groups", "seq"), None, None)
    return jax.shard_map(
        local,
        mesh=mesh,
        in_specs=(split,) * 4 + (P(),) * 3,
        out_specs=(split,) * 4,
        check_vma=False,
    )
```

```python
import functools

import jax
import jax.numpy as jnp
from jax import lax
from jax.experimental import pallas as pl
from jax.experimental.pallas import tpu as pltpu
from jax.sharding import PartitionSpec as P

DIGIT = 4


def exchange(x, mask):
    size = lax.axis_size("seq")
    return lax.ppermute(x, "seq", [(i, i ^ mask) for i in range(size)])


def route(x, mask):
    bits = lax.axis_size("seq").bit_length() - 1
    for low in range(0, bits, DIGIT):
        width = min(DIGIT, bits - low)
        digit = jnp.bitwise_and(jnp.right_shift(mask, low), (1 << width) - 1)
        moves = [lambda t: t] + [
            lambda t, m=value << low: exchange(t, m) for value in range(1, 1 << width)
        ]
        x = lax.switch(digit, moves, x)
    return x


def route_beside(x, mask, work, operand):
    bits = lax.axis_size("seq").bit_length() - 1
    if bits > DIGIT:
        return route(x, mask), work(operand)
    moves = [
        lambda t, o, m=value: (exchange(t, m) if m else t, work(o)) for value in range(1 << bits)
    ]
    return lax.switch(mask, moves, x, operand)


def bit_of(x, bit):
    return jnp.bitwise_and(jnp.right_shift(x, bit), 1)


def higher_bits():
    bits = lax.axis_size("seq").bit_length() - 1
    return list(range(bits - 1, 0, -1))


def fetch_global(own, source):
    me = lax.axis_index("seq")
    even = bit_of(me, 0) == 0
    kept = jnp.where(even, own[0], own[1])
    given = jnp.where(even, own[1], own[0])
    half = jnp.where(bit_of(me, 0) == bit_of(source, 0), kept, exchange(given, 1))
    for bit in higher_bits():
        other = exchange(half, 1 << bit)
        half = jnp.where(bit_of(me, bit) == bit_of(source, bit), half, other)
    other = exchange(half, 1)
    return jnp.stack([jnp.where(even, half, other), jnp.where(even, other, half)])


def reduce_global(terms, target):
    me = lax.axis_index("seq")
    even = bit_of(me, 0) == 0
    kept = jnp.where(even, terms[0], terms[1])
    given = jnp.where(even, terms[1], terms[0])
    half = kept + exchange(given.astype(jnp.bfloat16), 1).astype(jnp.float32)
    for bit in higher_bits():
        other = exchange(half.astype(jnp.bfloat16), 1 << bit).astype(jnp.float32)
        half = half + jnp.where(bit_of(me, bit) == bit_of(target, bit), other, 0.0)
    other = exchange(half.astype(jnp.bfloat16), 1).astype(jnp.float32)
    total = jnp.stack([jnp.where(even, half, other), jnp.where(even, other, half)])
    return jnp.where(me == target, total, 0.0)


def attention_kernel(
    near_count, which_ref, q_ref, g_ref, own_ref, far_ref, rand_ref, glob_ref, *rest
):
    near_refs = rest[:near_count]
    out_ref, dq_ref, own_t, far_t, near_t, rand_t, glob_t = rest[near_count:]
    group, rows, width = q_ref.shape
    scale = width**-0.5
    which = which_ref[0]

    def listed(side):
        near = near_refs[0][side, 0]
        for bit in range(1, near_count):
            near = jnp.where(which == bit, near_refs[bit][side, 0], near)
        return jnp.concatenate(
            [own_ref[side, 0], far_ref[side, 0], near, rand_ref[side, 0], glob_ref[side, 0]]
        )

    keys, values = listed(0), listed(1)
    q = q_ref[...].reshape(group * rows, width)
    g = g_ref[...].reshape(group * rows, width)
    contract_last = (((1,), (1,)), ((), ()))
    contract_first = (((0,), (0,)), ((), ()))
    scores = (
        lax.dot_general(keys, q, contract_last, preferred_element_type=jnp.float32) * scale
    )
    top = jnp.max(scores, axis=0, keepdims=True)
    weights = jnp.exp(scores - top)
    weights = weights * (1.0 / jnp.sum(weights, axis=0, keepdims=True))
    probs = weights.astype(jnp.bfloat16)
    out_t = lax.dot_general(values, probs, contract_first, preferred_element_type=jnp.float32)
    out = out_t.T.astype(jnp.bfloat16)
    out_ref[...] = out.reshape(group, rows, width)
    deltas = jnp.sum(
        g.T.astype(jnp.float32) * out_t.astype(jnp.bfloat16).astype(jnp.float32),
        axis=0,
        keepdims=True,
    )
    grad_probs = lax.dot_general(values, g, contract_last, preferred_element_type=jnp.float32)
    grad_scores = (weights * (grad_probs - deltas)).astype(jnp.bfloat16)
    dq_t = lax.dot_general(keys, grad_scores, contract_first, preferred_element_type=jnp.float32)
    dq_ref[...] = (dq_t * scale).T.astype(jnp.bfloat16).reshape(group, rows, width)
    key_terms = jnp.dot(grad_scores, q, preferred_element_type=jnp.float32) * scale
    value_terms = jnp.dot(probs, g, preferred_element_type=jnp.float32)
    for place, ref in enumerate((own_t, far_t, near_t, rand_t, glob_t)):
        part = slice(place * rows, (place + 1) * rows)
        ref[0, 0] = key_terms[part].astype(ref.dtype)
        ref[1, 0] = value_terms[part].astype(ref.dtype)


def attention(which, q, g, own, far, rand, glob, near):
    heads, rows, width = q.shape
    kv_count = own.shape[1]
    group = heads // kv_count
    by_query = pl.BlockSpec((group, rows, width), lambda h, *_: (h, 0, 0))
    by_key = pl.BlockSpec((2, 1, rows, width), lambda h, *_: (0, h, 0, 0))
    queries = jax.ShapeDtypeStruct(q.shape, q.dtype)
    exact = jax.ShapeDtypeStruct(own.shape, jnp.float32)
    sent = jax.ShapeDtypeStruct(own.shape, jnp.bfloat16)
    flops = 12 * heads * rows * 5 * rows * width
    return pl.pallas_call(
        functools.partial(attention_kernel, len(near)),
        grid_spec=pltpu.PrefetchScalarGridSpec(
            num_scalar_prefetch=1,
            grid=(kv_count,),
            in_specs=[by_query] * 2 + [by_key] * (4 + len(near)),
            out_specs=[by_query] * 2 + [by_key] * 5,
        ),
        out_shape=[queries, queries, exact, sent, sent, sent, exact],
        cost_estimate=pl.CostEstimate(
            flops=flops, bytes_accessed=8 * q.size, transcendentals=5 * rows * rows * heads
        ),
        name="attention",
    )(which, q, g, own, far, rand, glob, *near)


def local(queries, key_heads, value_heads, grad_out, offsets, random_masks, global_blocks):
    size = lax.axis_size("seq")
    me = lax.axis_index("seq")
    half = size // 2
    near_bits = size.bit_length() - 2
    other = jnp.where(offsets[0] == half, offsets[1], offsets[0])
    which = sum((other >= (2 << bit)).astype(jnp.int32) for bit in range(near_bits))
    mask, source = random_masks[0], global_blocks[0]

    own = jnp.stack([key_heads, value_heads]).transpose(0, 2, 1, 3)
    far = exchange(own, half)
    near = [exchange(own, 1 << bit) for bit in range(near_bits)]
    rand, glob = route_beside(own, mask, lambda t: fetch_global(t, source), own)
    q = queries.transpose(1, 0, 2)
    g = grad_out.transpose(1, 0, 2)
    out, dq, own_t, far_t, near_t, rand_t, glob_t = attention(
        which[None], q, g, own, far, rand, glob, near
    )
    rand_in, glob_in = route_beside(
        rand_t, mask, lambda t: reduce_global(t, source), glob_t
    )
    far_in = exchange(far_t, half)
    near_in = [exchange(near_t, 1 << bit) for bit in range(near_bits)]
    picked = near_in[0]
    for bit in range(1, near_bits):
        picked = jnp.where(which == bit, near_in[bit], picked)
    totals = own_t + glob_in
    for part in (far_in, picked, rand_in):
        totals = totals + part.astype(jnp.float32)
    grads = totals.astype(jnp.bfloat16).transpose(0, 2, 1, 3)
    return (out.transpose(1, 0, 2), dq.transpose(1, 0, 2), grads[0], grads[1])


def solution(mesh):
    split = P(("groups", "seq"), None, None)
    return jax.shard_map(
        local,
        mesh=mesh,
        in_specs=(split,) * 4 + (P(),) * 3,
        out_specs=(split,) * 4,
        check_vma=False,
    )
```

```python
import functools

import jax
import jax.numpy as jnp
from jax import lax
from jax.experimental import pallas as pl
from jax.experimental.pallas import tpu as pltpu
from jax.sharding import PartitionSpec as P


DIGIT = 4


def exchange(x, mask):
    size = lax.axis_size("seq")
    return lax.ppermute(x, "seq", [(i, i ^ mask) for i in range(size)])


def route(x, mask):
    bits = lax.axis_size("seq").bit_length() - 1
    for low in range(0, bits, DIGIT):
        width = min(DIGIT, bits - low)
        digit = jnp.bitwise_and(jnp.right_shift(mask, low), (1 << width) - 1)
        moves = [lambda t: t] + [
            lambda t, m=value << low: exchange(t, m) for value in range(1, 1 << width)
        ]
        x = lax.switch(digit, moves, x)
    return x


def bit_of(x, bit):
    return jnp.bitwise_and(jnp.right_shift(x, bit), 1)


def higher_bits():
    bits = lax.axis_size("seq").bit_length() - 1
    return list(range(bits - 1, 0, -1))


def core_halves(pair, even):
    return jnp.where(even, pair[0], pair[1]), jnp.where(even, pair[1], pair[0])


def fetch_global(own, source):
    me = lax.axis_index("seq")
    even = bit_of(me, 0) == 0
    kept, given = core_halves(own, even)
    half = jnp.where(bit_of(me, 0) == bit_of(source, 0), kept, exchange(given, 1))
    for bit in higher_bits():
        other = exchange(half, 1 << bit)
        half = jnp.where(bit_of(me, bit) == bit_of(source, bit), half, other)
    other = exchange(half, 1)
    return jnp.stack([jnp.where(even, half, other), jnp.where(even, other, half)])


def reduce_global(terms, target):
    me = lax.axis_index("seq")
    even = bit_of(me, 0) == 0
    kept, given = core_halves(terms, even)
    half = kept + exchange(given.astype(jnp.bfloat16), 1).astype(jnp.float32)
    for bit in higher_bits():
        other = exchange(half.astype(jnp.bfloat16), 1 << bit).astype(jnp.float32)
        half = half + jnp.where(bit_of(me, bit) == bit_of(target, bit), other, 0.0)
    other = exchange(half.astype(jnp.bfloat16), 1).astype(jnp.float32)
    return jnp.stack([jnp.where(even, half, other), jnp.where(even, other, half)])


def chips_apart(device):
    apart = jnp.bitwise_xor(lax.axis_index("seq"), device)
    return sum(bit_of(apart, bit) for bit in higher_bits())


def spread_global(near_block, source):
    me = lax.axis_index("seq")
    even = bit_of(me, 0) == 0
    kept, given = core_halves(near_block, even)
    other = exchange(given, 1)
    half = jnp.where(bit_of(me, 0) == bit_of(source, 0), kept, other)
    other = exchange(half, lax.axis_size("seq") - 2)
    half = jnp.where(chips_apart(source) <= 1, half, other)
    other = exchange(half, 1)
    return jnp.stack([jnp.where(even, half, other), jnp.where(even, other, half)])


def gather_global(terms, target):
    even = bit_of(lax.axis_index("seq"), 0) == 0
    kept, given = core_halves(terms, even)
    other = exchange(given.astype(jnp.bfloat16), 1)
    half = kept + other.astype(jnp.float32)
    other = exchange(half.astype(jnp.bfloat16), lax.axis_size("seq") - 2)
    half = half + jnp.where(chips_apart(target) <= 1, other.astype(jnp.float32), 0.0)
    other = exchange(half.astype(jnp.bfloat16), 1).astype(jnp.float32)
    return jnp.stack([jnp.where(even, half, other), jnp.where(even, other, half)])


def beside_moves(x, mask, work, *operands):
    def branch(value, x, *operands):
        moved = exchange(x, value) if value else x
        return moved, work(*operands)

    bits = lax.axis_size("seq").bit_length() - 2
    moves = [functools.partial(branch, value) for value in range(1 << bits)]
    return lax.switch(mask, moves, x, *operands)


def attention_kernel(
    near_count, which_ref, q_ref, g_ref, own_ref, far_ref, rand_ref, glob_ref, *rest
):
    near_refs = rest[:near_count]
    out_ref, dq_ref, own_t, far_t, near_t, rand_t, glob_t = rest[near_count:]
    group, rows, width = q_ref.shape
    scale = width**-0.5
    which = which_ref[0]

    def listed(side):
        near = near_refs[0][side, 0]
        for bit in range(1, near_count):
            near = jnp.where(which == bit, near_refs[bit][side, 0], near)
        return jnp.concatenate(
            [own_ref[side, 0], far_ref[side, 0], near, rand_ref[side, 0], glob_ref[side, 0]]
        )

    keys, values = listed(0), listed(1)
    q = q_ref[...].reshape(group * rows, width)
    g = g_ref[...].reshape(group * rows, width)
    contract_last = (((1,), (1,)), ((), ()))
    contract_first = (((0,), (0,)), ((), ()))
    scores = (
        lax.dot_general(keys, q, contract_last, preferred_element_type=jnp.float32) * scale
    )
    top = jnp.max(scores, axis=0, keepdims=True)
    weights = jnp.exp(scores - top)
    weights = weights * (1.0 / jnp.sum(weights, axis=0, keepdims=True))
    probs = weights.astype(jnp.bfloat16)
    out_t = lax.dot_general(values, probs, contract_first, preferred_element_type=jnp.float32)
    out = out_t.T.astype(jnp.bfloat16)
    out_ref[...] = out.reshape(group, rows, width)
    deltas = jnp.sum(
        g.T.astype(jnp.float32) * out_t.astype(jnp.bfloat16).astype(jnp.float32),
        axis=0,
        keepdims=True,
    )
    grad_probs = lax.dot_general(values, g, contract_last, preferred_element_type=jnp.float32)
    grad_scores = (weights * (grad_probs - deltas)).astype(jnp.bfloat16)
    dq_t = lax.dot_general(keys, grad_scores, contract_first, preferred_element_type=jnp.float32)
    dq_ref[...] = (dq_t * scale).T.astype(jnp.bfloat16).reshape(group, rows, width)
    key_terms = jnp.dot(grad_scores, q, preferred_element_type=jnp.float32) * scale
    value_terms = jnp.dot(probs, g, preferred_element_type=jnp.float32)
    for place, ref in enumerate((own_t, far_t, near_t, rand_t, glob_t)):
        part = slice(place * rows, (place + 1) * rows)
        ref[0, 0] = key_terms[part].astype(ref.dtype)
        ref[1, 0] = value_terms[part].astype(ref.dtype)


def attention(which, q, g, own, far, rand, glob, near):
    heads, rows, width = q.shape
    kv_count = own.shape[1]
    group = heads // kv_count
    by_query = pl.BlockSpec((group, rows, width), lambda h, *_: (h, 0, 0))
    by_key = pl.BlockSpec((2, 1, rows, width), lambda h, *_: (0, h, 0, 0))
    queries = jax.ShapeDtypeStruct(q.shape, q.dtype)
    exact = jax.ShapeDtypeStruct(own.shape, jnp.float32)
    sent = jax.ShapeDtypeStruct(own.shape, jnp.bfloat16)
    flops = 12 * heads * rows * 5 * rows * width
    return pl.pallas_call(
        functools.partial(attention_kernel, len(near)),
        grid_spec=pltpu.PrefetchScalarGridSpec(
            num_scalar_prefetch=1,
            grid=(kv_count,),
            in_specs=[by_query] * 2 + [by_key] * (4 + len(near)),
            out_specs=[by_query] * 2 + [by_key] * 5,
        ),
        out_shape=[queries, queries, exact, sent, sent, sent, exact],
        cost_estimate=pl.CostEstimate(
            flops=flops, bytes_accessed=8 * q.size, transcendentals=5 * rows * rows * heads
        ),
        name="attention",
    )(which, q, g, own, far, rand, glob, *near)


def local(queries, key_heads, value_heads, grad_out, offsets, random_masks, global_blocks):
    size = lax.axis_size("seq")
    me = lax.axis_index("seq")
    half = size // 2
    near_bits = size.bit_length() - 2
    other = jnp.where(offsets[0] == half, offsets[1], offsets[0])
    which = sum((other >= (2 << bit)).astype(jnp.int32) for bit in range(near_bits))
    mask, source = random_masks[0], global_blocks[0]

    short = size.bit_length() - 1 <= DIGIT
    low_mask, crossing = jnp.bitwise_and(mask, half - 1), mask >= half
    apart = jnp.bitwise_xor(me, source)

    own = jnp.stack([key_heads, value_heads]).transpose(0, 2, 1, 3)
    far = exchange(own, half)
    near = [exchange(own, 1 << bit) for bit in range(near_bits)]
    q = queries.transpose(1, 0, 2)
    g = grad_out.transpose(1, 0, 2)
    moving = jnp.where(crossing, far, own)
    if short:
        hold = own
        for bit in range(1, near_bits):
            hold = jnp.where(apart >> 1 == 1 << bit >> 1, near[bit], hold)
        hold = jnp.where(apart >> 1 == half >> 1, far, hold)
        moving, hold, q, g = lax.optimization_barrier((moving, hold, q, g))
        rand, glob = beside_moves(
            moving, low_mask, lambda t: spread_global(t, source), hold
        )
    else:
        rand, glob = route(moving, low_mask), fetch_global(own, source)
    out, dq, own_t, far_t, near_t, rand_t, glob_t = attention(
        which[None], q, g, own, far, rand, glob, near
    )
    if short:
        rand_in, glob_in = beside_moves(
            rand_t, low_mask, lambda t: gather_global(t, source), glob_t
        )
    else:
        rand_in, glob_in = route(rand_t, low_mask), reduce_global(glob_t, source)
    rand_in = rand_in.astype(jnp.float32)

    def toward(bit, terms):
        terms = terms.astype(jnp.float32)
        if short and bit:
            terms = terms + jnp.where(apart == 1 << bit, glob_in, 0.0)
        return exchange(terms.astype(jnp.bfloat16), 1 << bit).astype(jnp.float32)

    totals = toward(near_bits, far_t.astype(jnp.float32) + jnp.where(crossing, rand_in, 0.0))
    for bit in range(near_bits):
        totals = totals + toward(bit, jnp.where(which == bit, near_t, 0.0))
    totals = totals + own_t + jnp.where(crossing, 0.0, rand_in)
    totals = totals + jnp.where(apart == 0, glob_in, 0.0)
    grads = totals.astype(jnp.bfloat16).transpose(0, 2, 1, 3)
    return (out.transpose(1, 0, 2), dq.transpose(1, 0, 2), grads[0], grads[1])


def solution(mesh):
    split = P(("groups", "seq"), None, None)
    return jax.shard_map(
        local,
        mesh=mesh,
        in_specs=(split,) * 4 + (P(),) * 3,
        out_specs=(split,) * 4,
        check_vma=False,
    )
```

```python
import functools
import math

import jax
import jax.numpy as jnp
from jax import lax
from jax.experimental import pallas as pl
from jax.experimental.pallas import tpu as pltpu
from jax.sharding import PartitionSpec as P


DIGIT = 4


def exchange(x, mask):
    size = lax.axis_size("seq")
    return lax.ppermute(x, "seq", [(i, i ^ mask) for i in range(size)])


def route(x, mask):
    bits = lax.axis_size("seq").bit_length() - 1
    for low in range(0, bits, DIGIT):
        width = min(DIGIT, bits - low)
        digit = jnp.bitwise_and(jnp.right_shift(mask, low), (1 << width) - 1)
        moves = [lambda t: t] + [
            lambda t, m=value << low: exchange(t, m) for value in range(1, 1 << width)
        ]
        x = lax.switch(digit, moves, x)
    return x


def bit_of(x, bit):
    return jnp.bitwise_and(jnp.right_shift(x, bit), 1)


def higher_bits():
    bits = lax.axis_size("seq").bit_length() - 1
    return list(range(bits - 1, 0, -1))


def core_halves(pair, even):
    return jnp.where(even, pair[0], pair[1]), jnp.where(even, pair[1], pair[0])


def fetch_global(own, source):
    me = lax.axis_index("seq")
    even = bit_of(me, 0) == 0
    kept, given = core_halves(own, even)
    half = jnp.where(bit_of(me, 0) == bit_of(source, 0), kept, exchange(given, 1))
    for bit in higher_bits():
        other = exchange(half, 1 << bit)
        half = jnp.where(bit_of(me, bit) == bit_of(source, bit), half, other)
    other = exchange(half, 1)
    return jnp.stack([jnp.where(even, half, other), jnp.where(even, other, half)])


def reduce_global(terms, target):
    me = lax.axis_index("seq")
    even = bit_of(me, 0) == 0
    kept, given = core_halves(terms, even)
    half = kept + exchange(given.astype(jnp.bfloat16), 1).astype(jnp.float32)
    for bit in higher_bits():
        other = exchange(half.astype(jnp.bfloat16), 1 << bit).astype(jnp.float32)
        half = half + jnp.where(bit_of(me, bit) == bit_of(target, bit), other, 0.0)
    other = exchange(half.astype(jnp.bfloat16), 1).astype(jnp.float32)
    return jnp.stack([jnp.where(even, half, other), jnp.where(even, other, half)])


def chips_apart(device):
    apart = jnp.bitwise_xor(lax.axis_index("seq"), device)
    return sum(bit_of(apart, bit) for bit in higher_bits())


def spread_global(near_block, source):
    me = lax.axis_index("seq")
    even = bit_of(me, 0) == 0
    kept, given = core_halves(near_block, even)
    other = exchange(given, 1)
    half = jnp.where(bit_of(me, 0) == bit_of(source, 0), kept, other)
    other = exchange(half, lax.axis_size("seq") - 2)
    half = jnp.where(chips_apart(source) <= 1, half, other)
    other = exchange(half, 1)
    return jnp.stack([jnp.where(even, half, other), jnp.where(even, other, half)])


def gather_global(terms, target):
    even = bit_of(lax.axis_index("seq"), 0) == 0
    kept, given = core_halves(terms, even)
    other = exchange(given.astype(jnp.bfloat16), 1)
    half = kept + other.astype(jnp.float32)
    other = exchange(half.astype(jnp.bfloat16), lax.axis_size("seq") - 2)
    half = half + jnp.where(chips_apart(target) <= 1, other.astype(jnp.float32), 0.0)
    other = exchange(half.astype(jnp.bfloat16), 1).astype(jnp.float32)
    return jnp.stack([jnp.where(even, half, other), jnp.where(even, other, half)])


def beside_moves(x, mask, work, *operands):
    def branch(value, x, *operands):
        moved = exchange(x, value) if value else x
        return moved, work(*operands)

    bits = lax.axis_size("seq").bit_length() - 2
    moves = [functools.partial(branch, value) for value in range(1 << bits)]
    return lax.switch(mask, moves, x, *operands)


LAST = (((1,), (1,)), ((), ()))
FIRST = (((0,), (0,)), ((), ()))
TOGETHER = 2


def matmul(a, b, dims=(((1,), (0,)), ((), ()))):
    return lax.dot_general(a, b, dims, preferred_element_type=jnp.float32)


def attention_kernel(
    near_count, which_ref, q_ref, g_ref, own_ref, far_ref, rand_ref, glob_ref, *rest
):
    near_refs = rest[:near_count]
    out_ref, dq_ref = rest[near_count : near_count + 2]
    term_refs = rest[near_count + 2 :]
    rows, width = q_ref.shape[1:]
    group = q_ref.shape[0] // TOGETHER
    scale = width**-0.5
    heads = range(TOGETHER)

    def listed(side, h):
        near = near_refs[0][side, h]
        for bit in range(1, near_count):
            near = jnp.where(which_ref[0] == bit, near_refs[bit][side, h], near)
        return jnp.concatenate(
            [own_ref[side, h], far_ref[side, h], near, rand_ref[side, h], glob_ref[side, h]]
        )

    def of_queries(ref, h):
        return ref[h * group : (h + 1) * group].reshape(group * rows, width)

    def put_queries(ref, h, x):
        ref[h * group : (h + 1) * group] = x.astype(ref.dtype).reshape(group, rows, width)

    def put_terms(side, h, terms):
        for place, ref in enumerate(term_refs):
            ref[side, h] = terms[place * rows : (place + 1) * rows].astype(ref.dtype)

    q, g = [of_queries(q_ref, h) for h in heads], [of_queries(g_ref, h) for h in heads]
    keys = [listed(0, h) for h in heads]
    scores = [matmul(keys[h], q[h], LAST) * (math.log2(math.e) * scale) for h in heads]
    weights = []
    for h in heads:
        raised = jnp.exp2(scores[h] - jnp.max(scores[h], axis=0, keepdims=True))
        weights.append(raised * (1.0 / jnp.sum(raised, axis=0, keepdims=True)))
    probs = [weights[h].astype(jnp.bfloat16) for h in heads]
    values = [listed(1, h) for h in heads]
    grad_probs = [matmul(values[h], g[h], LAST) for h in heads]
    outs = [matmul(values[h], probs[h], FIRST) for h in heads]
    deltas = []
    for h in heads:
        put_queries(out_ref, h, outs[h].T)
        rounded = outs[h].astype(jnp.bfloat16).astype(jnp.float32)
        deltas.append(jnp.sum(g[h].T.astype(jnp.float32) * rounded, axis=0, keepdims=True))
    grad_scores = [(weights[h] * (grad_probs[h] - deltas[h])).astype(jnp.bfloat16) for h in heads]
    for h in heads:
        put_terms(1, h, matmul(probs[h], g[h]))
    for h in heads:
        put_queries(dq_ref, h, (matmul(keys[h], grad_scores[h], FIRST) * scale).T)
        put_terms(0, h, matmul(grad_scores[h], q[h]) * scale)


def attention(which, q, g, own, far, rand, glob, near):
    heads, rows, width = q.shape
    kv_count = own.shape[1]
    group = heads // kv_count * TOGETHER
    by_query = pl.BlockSpec((group, rows, width), lambda h, *_: (h, 0, 0))
    by_key = pl.BlockSpec((2, TOGETHER, rows, width), lambda h, *_: (0, h, 0, 0))
    queries = jax.ShapeDtypeStruct(q.shape, q.dtype)
    exact = jax.ShapeDtypeStruct(own.shape, jnp.float32)
    sent = jax.ShapeDtypeStruct(own.shape, jnp.bfloat16)
    flops = 12 * heads * rows * 5 * rows * width
    return pl.pallas_call(
        functools.partial(attention_kernel, len(near)),
        grid_spec=pltpu.PrefetchScalarGridSpec(
            num_scalar_prefetch=1,
            grid=(kv_count // TOGETHER,),
            in_specs=[by_query] * 2 + [by_key] * (4 + len(near)),
            out_specs=[by_query] * 2 + [by_key] * 5,
        ),
        out_shape=[queries, queries, exact, sent, sent, sent, exact],
        cost_estimate=pl.CostEstimate(
            flops=flops, bytes_accessed=8 * q.size, transcendentals=5 * rows * rows * heads
        ),
        name="attention",
    )(which, q, g, *[pltpu.with_memory_space_constraint(x, pltpu.VMEM) for x in (own, far, rand, glob, *near)])


def local(queries, key_heads, value_heads, grad_out, offsets, random_masks, global_blocks):
    size = lax.axis_size("seq")
    me = lax.axis_index("seq")
    half = size // 2
    near_bits = size.bit_length() - 2
    other = jnp.where(offsets[0] == half, offsets[1], offsets[0])
    which = sum((other >= (2 << bit)).astype(jnp.int32) for bit in range(near_bits))
    mask, source = random_masks[0], global_blocks[0]

    short = size.bit_length() - 1 <= DIGIT
    low_mask, crossing = jnp.bitwise_and(mask, half - 1), mask >= half
    apart = jnp.bitwise_xor(me, source)

    own = jnp.stack([key_heads, value_heads]).transpose(0, 2, 1, 3)
    far = exchange(own, half)
    near = [exchange(own, 1 << bit) for bit in range(near_bits)]
    q = queries.transpose(1, 0, 2)
    g = grad_out.transpose(1, 0, 2)
    moving = jnp.where(crossing, far, own)
    if short:
        hold = own
        for bit in range(1, near_bits):
            hold = jnp.where(apart >> 1 == 1 << bit >> 1, near[bit], hold)
        hold = jnp.where(apart >> 1 == half >> 1, far, hold)
        moving, hold, q, g = lax.optimization_barrier((moving, hold, q, g))
        rand, glob = beside_moves(
            moving, low_mask, lambda t: spread_global(t, source), hold
        )
    else:
        rand, glob = route(moving, low_mask), fetch_global(own, source)
    out, dq, own_t, far_t, near_t, rand_t, glob_t = attention(
        which[None], q, g, own, far, rand, glob, near
    )
    if short:
        rand_in, glob_in = beside_moves(
            rand_t, low_mask, lambda t: gather_global(t, source), glob_t
        )
    else:
        rand_in, glob_in = route(rand_t, low_mask), reduce_global(glob_t, source)
    rand_in = rand_in.astype(jnp.float32)

    def toward(bit, terms):
        terms = terms.astype(jnp.float32)
        if short and bit:
            terms = terms + jnp.where(apart == 1 << bit, glob_in, 0.0)
        return exchange(terms.astype(jnp.bfloat16), 1 << bit).astype(jnp.float32)

    totals = toward(near_bits, far_t.astype(jnp.float32) + jnp.where(crossing, rand_in, 0.0))
    for bit in range(near_bits):
        totals = totals + toward(bit, jnp.where(which == bit, near_t, 0.0))
    totals = totals + own_t + jnp.where(crossing, 0.0, rand_in)
    totals = totals + jnp.where(apart == 0, glob_in, 0.0)
    grads = totals.astype(jnp.bfloat16).transpose(0, 2, 1, 3)
    return (out.transpose(1, 0, 2), dq.transpose(1, 0, 2), grads[0], grads[1])


def solution(mesh):
    split = P(("groups", "seq"), None, None)
    return jax.shard_map(
        local,
        mesh=mesh,
        in_specs=(split,) * 4 + (P(),) * 3,
        out_specs=(split,) * 4,
        check_vma=False,
    )
```
